32 devices in a mesh: groups: 2 (over x), dev: 16 (over z, y, core).
Axes of the slice: x: 2, y: 2, z: 4, core: 2. Of those that a mesh axis runs over, the one named last changes fastest.
Arguments:
- residual: bfloat16 [64, 7168], P(('groups', 'dev')), parts along dimension 0, may hold values from -6 to 6
- queries: bfloat16 [64, 16384], P(('groups', 'dev')), parts along dimension 0, may hold values from -512 to 512
- key_cache: bfloat16 [64, 512, 256], P(('groups', 'dev')), parts along dimension 0, may hold values from -8 to 8
- value_cache: bfloat16 [64, 512, 256], P(('groups', 'dev')), parts along dimension 0, may hold values from -6 to 6
- key_new: bfloat16 [64, 256], P(('groups', 'dev')), parts along dimension 0, may hold values from -6 to 6
- value_new: bfloat16 [64, 256], P(('groups', 'dev')), parts along dimension 0, may hold values from -6 to 6
- lengths: int32 [64], P(('groups', 'dev')), parts along dimension 0, may hold values from 2 to 512
- out_weight: bfloat16 [16384, 7168], P('dev'), may hold values from -0.375 to 0.375
- norm_gain: bfloat16 [7168], replicated, may hold values from 0.25 to 1.75
- shared_up: bfloat16 [7168, 5120], P(None, 'dev'), may hold values from -0.0625 to 0.0625
- shared_down: bfloat16 [5120, 7168], P('dev'), may hold values from -0.15625 to 0.15625
- expert_up: bfloat16 [7168, 10240], P(None, 'dev'), may hold values from -0.0625 to 0.0625
- expert_down: bfloat16 [10240, 7168], P('dev'), may hold values from -0.25 to 0.25
- expert_ids: int32 [64, 3], P(('groups', 'dev')), parts along dimension 0, may hold values from 0 to 3, all different within a row
- expert_gates: float32 [64, 3], P(('groups', 'dev')), parts along dimension 0, may hold values from 0.1 to 1
Outputs:
- mixed: bfloat16 [64, 7168], P(('groups', 'dev')), parts along dimension 0
The draws below stay inside these ranges and needn't reach their ends.
There are 2 independent parts, one for each index of `groups`. The reference program is written for one: setup_inputs(seed, part) draws one part's arguments, and reference() takes and returns one part's arrays. A program takes and returns all parts, laid end to end along the dimension named above; an argument that names none is the same for every part. Nothing has to cross between parts.
Inputs may be any that keep to these rules, and one draw needn't show every extreme that they name: `expert_ids`: each row names 3 different experts.
All inputs are finite; a program needn't handle non-finite values.
Results may differ from the reference program's by a relative error of at most 0.008.
Values may be sent and summed in bfloat16 or wider, within the bound.
A program may use at most 128 MiB of HBM per device.

```python
import math
import jax
import jax.numpy as jnp
from jax import lax

D = 7168
HEADS = 64
HEAD_DIM = 256
SHARED = 5120
EXPERT_FF = 2560
EXPERTS = 4
TOP = 3
LEN = 512
ROWS = 32


def common_keys(key):
    base = jax.random.fold_in(key, 7)
    keys_drawn = jax.random.normal(base, (ROWS, LEN, HEAD_DIM), jnp.float32)
    return jnp.clip(keys_drawn, -8.0, 8.0)


def draw_key_cache(key, part):
    return common_keys(key).astype(jnp.bfloat16)


def draw_queries(key, part):
    drawn = jax.random.normal(jax.random.fold_in(key, 17), (ROWS, HEADS * HEAD_DIM), jnp.float32)
    return drawn.astype(jnp.bfloat16)


def touch_ends(values, stream_key, low, largest):
    shape = values.shape
    spot = [jax.random.randint(jax.random.fold_in(stream_key, axis), (), 0, shape[axis]) for axis in range(len(shape))]
    values = values.at[tuple(spot)].set(low)
    longest = shape.index(max(shape))
    spot[longest] = (spot[longest] + 1) % shape[longest]
    return values.at[tuple(spot)].set(largest)


def block_levels(rng, extent, shards, low, top_value):
    level = 1.0
    for axis_at, parts in shards:
        steps = jax.random.uniform(jax.random.fold_in(jax.random.fold_in(rng, 6), axis_at), (parts,), jnp.float32, low / len(shards), top_value / len(shards))
        level = level * jnp.repeat(jnp.exp(steps), extent[axis_at] // parts).reshape((-1,) + (1,) * (len(extent) - 1 - axis_at))
    return level


def picks_of(stream_key, rows, amount, top, lift):
    sequence = jax.random.permutation(jax.random.fold_in(stream_key, 1), amount)
    pull = sequence
    for power in range(3):
        pull = pull * pull // amount
    pull = pull * lift // amount
    chance = jax.random.randint(jax.random.fold_in(stream_key, 2), (rows, amount), 0, 4096) + pull
    fixed_rows = jax.random.permutation(jax.random.fold_in(stream_key, 3), rows)[jnp.arange(amount) % rows]
    chance = jnp.where(jnp.arange(rows)[:, None] == fixed_rows[None, :], 1 << 14, chance)
    merit = chance * amount + jnp.arange(amount)
    return lax.top_k(merit.astype(jnp.int32), top)[1].astype(jnp.int32)


def scatter_about(stream_key, extent, deviation, bound, split=(), kind=jnp.bfloat16):
    gain = block_levels(stream_key, extent, split, -0.22, 0.18) if split else 1.0
    entries = jax.random.normal(stream_key, extent, jnp.float32) * deviation * gain
    return jnp.minimum(jnp.maximum(entries, -bound), bound).astype(kind)


def setup_inputs(seed: int = 0, part: int = 0) -> dict:
    splits = jax.random.split(jax.random.key(seed), 16)
    part_keys = jax.random.split(jax.random.fold_in(splits[15], part), 16)
    return {
        "residual": scatter_about(part_keys[0], (ROWS, D), 1.0, 6.0, ((0, 16),)),
        "queries": draw_queries(jax.random.fold_in(jax.random.fold_in(splits[15], part), 71), part),
        "key_cache": draw_key_cache(jax.random.fold_in(jax.random.fold_in(splits[15], part), 71), part),
        "value_cache": scatter_about(part_keys[3], (ROWS, LEN, HEAD_DIM), 1.0, 6.0, ((0, 16),)),
        "key_new": scatter_about(part_keys[4], (ROWS, HEAD_DIM), 1.0, 6.0, ((0, 16),)),
        "value_new": scatter_about(part_keys[5], (ROWS, HEAD_DIM), 1.0, 6.0, ((0, 16),)),
        "lengths": touch_ends(jax.random.randint(part_keys[6], (ROWS,), 2, LEN + 1), jax.random.fold_in(part_keys[6], 1), 2, LEN).astype(jnp.int32),
        "out_weight": scatter_about(splits[7], (HEADS * HEAD_DIM, D), HEAD_DIM ** -0.5, 0.375, ((0, 16),)),
        "norm_gain": jnp.clip(1.0 + 0.15 * jax.random.normal(splits[8], (D,), jnp.float32), 0.25, 1.75).astype(jnp.bfloat16),
        "shared_up": scatter_about(splits[9], (D, SHARED), D ** -0.5, 0.0625, ((1, 16),)),
        "shared_down": scatter_about(splits[10], (SHARED, D), (SHARED // 4) ** -0.5, 0.15625, ((0, 16),)),
        "expert_up": scatter_about(splits[11], (D, EXPERTS * EXPERT_FF), D ** -0.5, 0.0625, ((1, 16),)),
        "expert_down": scatter_about(splits[12], (EXPERTS * EXPERT_FF, D), (EXPERT_FF // 4) ** -0.5, 0.25, ((0, 16),)),
        "expert_ids": picks_of(part_keys[13], ROWS, EXPERTS, TOP, 12000),
        "expert_gates": jnp.clip(0.1 + 0.9 * jax.random.uniform(part_keys[14], (ROWS, TOP), jnp.float32) ** block_levels(part_keys[14], (ROWS, TOP), ((0, 16),), -0.2, 0.2), 0.1, 1.0),
    }


def attend(queries, key_cache, value_cache, key_new, value_new, lengths):
    row_count = queries.shape[0]
    head_dim = key_cache.shape[2]
    factor = 1.0 / math.sqrt(head_dim)
    query_heads = queries.reshape(row_count, -1, head_dim).astype(jnp.float32)
    cached = jnp.einsum('rhd,rld->rhl', query_heads, key_cache.astype(jnp.float32)) * factor
    places = jnp.arange(key_cache.shape[1], dtype=jnp.int32)
    visible = places[None, None, :] < lengths[:, None, None]
    cached = jnp.where(visible, cached, -1e+30)
    own_score = jnp.einsum('rhd,rd->rh', query_heads, key_new.astype(jnp.float32)) * factor
    highest = jnp.maximum(lax.optimization_barrier(jnp.max(cached, axis=2)), own_score)
    raised = jnp.where(visible, jnp.exp(cached - highest[:, :, None]), 0.0)
    raised_new = jnp.exp(own_score - highest)
    denominator = lax.optimization_barrier(jnp.sum(raised, axis=2)) + raised_new
    weights = (raised / denominator[:, :, None]).astype(jnp.bfloat16)
    weights_new = (raised_new / denominator).astype(jnp.bfloat16)
    context = jnp.einsum('rhl,rld->rhd', weights.astype(jnp.float32), value_cache.astype(jnp.float32))
    context = context + weights_new.astype(jnp.float32)[:, :, None] * value_new.astype(jnp.float32)[:, None, :]
    return context.reshape(row_count, -1).astype(jnp.bfloat16)

def normalize(hidden, norm_gain):
    mean_square = lax.optimization_barrier(jnp.mean(hidden * hidden, axis=-1, keepdims=True))
    return (hidden * lax.rsqrt(mean_square + 1e-06) * norm_gain.astype(jnp.float32)).astype(jnp.bfloat16)

def reference(residual, queries, key_cache, value_cache, key_new, value_new, lengths, out_weight, norm_gain, shared_up, shared_down, expert_up, expert_down, expert_ids, expert_gates):
    context = attend(queries, key_cache, value_cache, key_new, value_new, lengths)
    hidden = residual.astype(jnp.float32) + jnp.dot(context, out_weight, preferred_element_type=jnp.float32)
    normed = normalize(hidden, norm_gain)
    shared_act = jax.nn.silu(jnp.dot(normed, shared_up, preferred_element_type=jnp.float32)).astype(jnp.bfloat16)
    mixed = hidden + jnp.dot(shared_act, shared_down, preferred_element_type=jnp.float32)
    for expert in range(EXPERTS):
        first_unit = expert * EXPERT_FF
        activation = jax.nn.silu(jnp.dot(normed, expert_up[:, first_unit:first_unit + EXPERT_FF], preferred_element_type=jnp.float32)).astype(jnp.bfloat16)
        weight = lax.optimization_barrier(jnp.sum(jnp.where(expert_ids == expert, expert_gates, jnp.zeros_like(expert_gates)), axis=1))
        mixed = mixed + weight[:, None] * jnp.dot(activation, expert_down[first_unit:first_unit + EXPERT_FF], preferred_element_type=jnp.float32)
    return mixed.astype(jnp.bfloat16)
```

```python
import functools
import math

import jax
import jax.numpy as jnp
from jax import lax
from jax.experimental import pallas as pl
from jax.experimental.pallas import tpu as pltpu
from jax.sharding import PartitionSpec as P

EXPERTS = 4
CHUNKS = 4
F32 = jnp.float32
BF16 = jnp.bfloat16


def layer_kernel(
    n,
    residual,
    queries,
    key_new,
    value_new,
    lengths,
    gain,
    ids,
    gates,
    key_hbm,
    value_hbm,
    out_hbm,
    sup_hbm,
    sdown_hbm,
    eup_hbm,
    edown_hbm,
    mixed,
    keys,
    values,
    out_w,
    sup_w,
    sdown_w,
    eup_w,
    edown_w,
    q_stage,
    c_stage,
    c_send,
    c_recv,
    g_recv,
    lhs_stage,
    g_stage,
    t_stage,
    s1a,
    r1a,
    s2a,
    r2a,
    s1b,
    r1b,
    s2b,
    r2b,
    own_total,
    hidden,
    normed,
    n_stage,
    load_sem,
    c_send_sem,
    c_recv_sem,
    g_send_sem,
    g_recv_sem,
    s1_sem,
    r1_sem,
    s2_sem,
    r2_sem,
    n_send_sem,
    n_recv_sem,
    f_send_sem,
    f_recv_sem,
):
    rows, width = residual.shape
    head_dim = keys.shape[2]
    heads = queries.shape[1] // head_dim
    per = heads // n
    chips = n // 2
    half = chips * rows
    total_rows = 2 * half
    chunk = width // CHUNKS
    me = lax.axis_index("dev")
    core = lax.rem(me, 2)
    chip = lax.div(me, 2)
    partner = me + 1 - 2 * core

    def cols(j):
        return pl.ds(j * chunk, chunk)

    def place(s):
        return (s % 2) * half + (s // 2) * rows

    loads = []
    for src, dst in (
        (key_hbm, keys),
        (value_hbm, values),
        (out_hbm, out_w),
        (sup_hbm, sup_w),
        (eup_hbm, eup_w),
        (sdown_hbm, sdown_w),
        (edown_hbm, edown_w),
    ):
        load = pltpu.make_async_copy(src, dst, load_sem.at[len(loads)])
        load.start()
        loads.append(load)

    barrier = pltpu.get_barrier_semaphore()

    def greet(o, carry):
        pl.semaphore_signal(
            barrier,
            inc=1,
            device_id={"dev": lax.rem(me + o, n)},
            device_id_type=pl.DeviceIdType.MESH,
        )
        return carry

    lax.fori_loop(1, n, greet, 0)

    def remote(src, dst, send, recv, device):
        return pltpu.make_async_remote_copy(
            src_ref=src,
            dst_ref=dst,
            send_sem=send,
            recv_sem=recv,
            device_id={"dev": device},
            device_id_type=pl.DeviceIdType.MESH,
        )

    lane = lax.broadcasted_iota(jnp.int32, (rows, 128), 1)
    table = jnp.zeros((rows, 128), F32)
    for k in range(ids.shape[1]):
        table = table + jnp.where(lane == ids[:, k : k + 1], gates[:, k : k + 1], 0.0)
    g_recv[pl.ds(me, 1)] = table[None]

    for h in range(heads):
        x = queries[:, h * head_dim : (h + 1) * head_dim].astype(F32)
        for r in range(rows):
            q_stage[r, h : h + 1, :] = x[r : r + 1]
    loads[0].wait()
    loads[1].wait()
    factor = 1.0 / math.sqrt(head_dim)
    for r in range(rows):
        q32 = q_stage[r]
        scores = (
            lax.dot_general(
                q32.astype(BF16), keys[r], (((1,), (1,)), ((), ())), preferred_element_type=F32
            )
            * factor
        )
        visible = lax.broadcasted_iota(jnp.int32, scores.shape, 1) < lengths[r]
        scores = jnp.where(visible, scores, -1e30)
        own = (
            jnp.sum(q32 * key_new[r : r + 1, :].astype(F32), axis=1, keepdims=True) * factor
        )
        top = jnp.maximum(jnp.max(scores, axis=1, keepdims=True), own)
        raised = jnp.where(visible, jnp.exp(scores - top), 0.0)
        raised_new = jnp.exp(own - top)
        denominator = jnp.sum(raised, axis=1, keepdims=True) + raised_new
        probs = (raised / denominator).astype(BF16)
        probs_new = (raised_new / denominator).astype(BF16).astype(F32)
        context = jnp.dot(probs, values[r], preferred_element_type=F32)
        context = context + probs_new * value_new[r : r + 1, :].astype(F32)
        q_stage[r] = context
    for d in range(n):
        for r in range(rows):
            c_stage[d, r * per : (r + 1) * per, :] = q_stage[r, d * per : (d + 1) * per, :]
    for d in range(n):
        c_send[d] = c_stage[d].astype(BF16)
    c_recv[pl.ds(me, 1)] = c_send[pl.ds(me, 1)]

    pl.semaphore_wait(barrier, n - 1)

    def c_copy(o):
        to = lax.rem(me + o, n)
        return remote(c_send.at[to], c_recv.at[me], c_send_sem, c_recv_sem.at[me], to)

    def g_copy(o):
        to = lax.rem(me + o, n)
        return remote(g_recv.at[me], g_recv.at[me], g_send_sem, g_recv_sem.at[me], to)

    for o in range(1, n):
        c_copy(o).start()
    for o in range(1, n):
        g_copy(o).start()
    for o in range(1, n):
        s = lax.rem(me + o, n)
        remote(c_recv.at[s], c_recv.at[s], c_send_sem, c_recv_sem.at[s], s).wait_recv()

    for s in range(n):
        x = c_recv[s].astype(F32)
        for r in range(rows):
            for h in range(per):
                lhs_stage[
                    place(s) + r : place(s) + r + 1, h * head_dim : (h + 1) * head_dim
                ] = x[r * per + h : r * per + h + 1]
    lhs = lhs_stage[...].astype(BF16)

    def first_stage(j, part, s1, r1, sem_at):
        part_a, part_b = part[:half], part[half:]
        s1[:, cols(j)] = jnp.where(core == 0, part_b, part_a).astype(BF16)
        copy = remote(
            s1.at[:, cols(j)],
            r1.at[:, cols(j)],
            s1_sem.at[sem_at, j],
            r1_sem.at[sem_at, j],
            partner,
        )
        copy.start()
        t_stage[:, cols(j)] = jnp.where(core == 0, part_a, part_b)
        return copy

    def second_copy(j, o, s2, r2, sem_at):
        to = lax.rem(chip + o, chips)
        return remote(
            s2.at[to, :, cols(j)],
            r2.at[chip, :, cols(j)],
            s2_sem.at[sem_at],
            r2_sem.at[sem_at, j, chip],
            2 * to + core,
        )

    def second_stage(j, copy, s2, r1, r2, sem_at):
        copy.wait_recv()
        t_stage[:, cols(j)] = t_stage[:, cols(j)] + r1[:, cols(j)].astype(F32)
        for c in range(chips):
            x = t_stage[c * rows : (c + 1) * rows, cols(j)]
            s2[c, :, cols(j)] = x.astype(BF16)
        for o in range(1, chips):
            second_copy(j, o, s2, r2, sem_at).start()

    def gathered(j, s2, r2, sem_at):
        x = s2[chip, :, cols(j)].astype(F32)
        for o in range(1, chips):
            c = lax.rem(chip + o, chips)
            remote(
                r2.at[c, :, cols(j)],
                r2.at[c, :, cols(j)],
                s2_sem.at[sem_at],
                r2_sem.at[sem_at, j, c],
                2 * c + core,
            ).wait_recv()
            x = x + r2[c, :, cols(j)].astype(F32)
        return x

    def reduce_scatter(make, s1, r1, s2, r2, sem_at):
        copies = []
        for j in range(CHUNKS):
            copies.append(first_stage(j, make(j), s1, r1, sem_at))
            if j >= 1:
                second_stage(j - 1, copies[j - 1], s2, r1, r2, sem_at)
        second_stage(CHUNKS - 1, copies[-1], s2, r1, r2, sem_at)

    loads[2].wait()
    reduce_scatter(
        lambda j: jnp.dot(lhs, out_w[:, cols(j)], preferred_element_type=F32), s1a, r1a, s2a, r2a, 0
    )

    square = jnp.zeros((rows, 1), F32)
    for j in range(CHUNKS):
        x = gathered(j, s2a, r2a, 0) + residual[:, cols(j)].astype(F32)
        hidden[:, cols(j)] = x
        square = square + jnp.sum(x * x, axis=1, keepdims=True)
    scale = lax.rsqrt(square / width + 1e-06)

    def n_copy(j, o):
        to = lax.rem(chip + o, chips)
        here = normed.at[core, chip, :, cols(j)]
        return remote(here, here, n_send_sem, n_recv_sem.at[j, chip], 2 * to + core)

    for j in range(CHUNKS):
        x = hidden[:, cols(j)] * scale * gain[:, cols(j)].astype(F32)
        normed[pl.ds(core, 1), pl.ds(chip, 1), :, cols(j)] = x.astype(BF16)[None, None]
        for o in range(1, chips):
            n_copy(j, o).start()

    for o in range(1, n):
        s = lax.rem(me + o, n)
        remote(g_recv.at[s], g_recv.at[s], g_send_sem, g_recv_sem.at[s], s).wait_recv()
    for s in range(n):
        g_stage[place(s) : place(s) + rows, :] = g_recv[s]
    owner = lax.div(me, n // EXPERTS)
    lanes = lax.broadcasted_iota(jnp.int32, (total_rows, 128), 1)
    row_weight = jnp.sum(jnp.where(lanes == owner, g_stage[...], 0.0), axis=1, keepdims=True)

    def forward(j):
        block = normed.at[core, :, :, cols(j)]
        return remote(block, block, f_send_sem.at[j], f_recv_sem.at[j], partner)

    def arrive(j):
        for o in range(1, chips):
            c = lax.rem(chip + o, chips)
            there = normed.at[core, c, :, cols(j)]
            remote(there, there, n_send_sem, n_recv_sem.at[j, c], 2 * c + core).wait_recv()
        forward(j).start()

    loads[3].wait()
    loads[4].wait()
    shared = jnp.zeros((total_rows, sup_w.shape[1]), F32)
    routed = jnp.zeros((total_rows, eup_w.shape[1]), F32)
    arrive(0)
    for j in range(CHUNKS):
        if j + 1 < CHUNKS:
            arrive(j + 1)
        other = normed.at[1 - core, :, :, cols(j)]
        remote(other, other, f_send_sem.at[j], f_recv_sem.at[j], partner).wait_recv()
        for s in range(n):
            n_stage[place(s) : place(s) + rows, :] = normed[s % 2, s // 2, :, cols(j)].astype(F32)
        left = n_stage[...].astype(BF16)
        shared = shared + jnp.dot(left, sup_w[cols(j), :], preferred_element_type=F32)
        routed = routed + jnp.dot(left, eup_w[cols(j), :], preferred_element_type=F32)

    shared_act = (shared / (1.0 + jnp.exp(-shared))).astype(BF16)
    routed_act = (routed / (1.0 + jnp.exp(-routed))).astype(BF16)

    loads[5].wait()
    loads[6].wait()
    reduce_scatter(
        lambda j: jnp.dot(shared_act, sdown_w[:, cols(j)], preferred_element_type=F32)
        + row_weight * jnp.dot(routed_act, edown_w[:, cols(j)], preferred_element_type=F32),
        s1b,
        r1b,
        s2b,
        r2b,
        1,
    )
    for j in range(CHUNKS):
        mixed[:, cols(j)] = (hidden[:, cols(j)] + gathered(j, s2b, r2b, 1)).astype(BF16)

    for o in range(1, n):
        c_copy(o).wait_send()
        g_copy(o).wait_send()
    for j in range(CHUNKS):
        forward(j).wait_send()
        for s1, r1, s2, r2, sem_at in ((s1a, r1a, s2a, r2a, 0), (s1b, r1b, s2b, r2b, 1)):
            remote(
                s1.at[:, cols(j)],
                r1.at[:, cols(j)],
                s1_sem.at[sem_at, j],
                r1_sem.at[sem_at, j],
                partner,
            ).wait_send()
            for o in range(1, chips):
                second_copy(j, o, s2, r2, sem_at).wait_send()
        for o in range(1, chips):
            n_copy(j, o).wait_send()


def shards(
    residual,
    queries,
    key_cache,
    value_cache,
    key_new,
    value_new,
    lengths,
    out_weight,
    norm_gain,
    shared_up,
    shared_down,
    expert_up,
    expert_down,
    expert_ids,
    expert_gates,
):
    n = lax.axis_size("dev")
    rows, width = residual.shape
    head_dim = key_cache.shape[2]
    heads = queries.shape[1] // head_dim
    per = heads // n
    chips = n // 2
    half = chips * rows
    chunk = width // CHUNKS
    vmem = pl.BlockSpec(memory_space=pltpu.VMEM)
    smem = pl.BlockSpec(memory_space=pltpu.SMEM)
    hbm = pl.BlockSpec(memory_space=pl.ANY)
    dma = pltpu.SemaphoreType.DMA
    stage_pair = [
        pltpu.VMEM((half, width), BF16),
        pltpu.VMEM((half, width), BF16),
        pltpu.VMEM((chips, rows, width), BF16),
        pltpu.VMEM((chips, rows, width), BF16),
    ]
    return pl.pallas_call(
        functools.partial(layer_kernel, n),
        out_shape=jax.ShapeDtypeStruct((rows, width), BF16),
        in_specs=[vmem] * 4 + [smem] + [vmem] * 3 + [hbm] * 7,
        out_specs=vmem,
        scratch_shapes=[
            pltpu.VMEM(a.shape, BF16)
            for a in (
                key_cache,
                value_cache,
                out_weight,
                shared_up,
                shared_down,
                expert_up,
                expert_down,
            )
        ]
        + [
            pltpu.VMEM((rows, heads, head_dim), F32),
            pltpu.VMEM((n, rows * per, head_dim), F32),
            pltpu.VMEM((n, rows * per, head_dim), BF16),
            pltpu.VMEM((n, rows * per, head_dim), BF16),
            pltpu.VMEM((n, rows, 128), F32),
            pltpu.VMEM((2 * half, per * head_dim), F32),
            pltpu.VMEM((2 * half, 128), F32),
            pltpu.VMEM((half, width), F32),
        ]
        + stage_pair
        + stage_pair
        + [
            pltpu.VMEM((rows, width), F32),
            pltpu.VMEM((rows, width), F32),
            pltpu.VMEM((2, chips, rows, width), BF16),
            pltpu.VMEM((2 * half, chunk), F32),
            dma((7,)),
            dma,
            dma((n,)),
            dma,
            dma((n,)),
            dma((2, CHUNKS)),
            dma((2, CHUNKS)),
            dma((2,)),
            dma((2, CHUNKS, chips)),
            dma,
            dma((CHUNKS, chips)),
            dma((CHUNKS,)),
            dma((CHUNKS,)),
        ],
        compiler_params=pltpu.CompilerParams(
            collective_id=0, has_side_effects=True, vmem_limit_bytes=63 * 1024 * 1024
        ),
        name="layer",
    )(
        residual,
        queries,
        key_new,
        value_new,
        lengths,
        norm_gain.reshape(1, -1),
        expert_ids,
        expert_gates,
        key_cache,
        value_cache,
        out_weight,
        shared_up,
        shared_down,
        expert_up,
        expert_down,
    )


def solution(mesh):
    return jax.shard_map(
        shards,
        mesh=mesh,
        in_specs=(
            P(("groups", "dev"), None),
            P(("groups", "dev"), None),
            P(("groups", "dev"), None, None),
            P(("groups", "dev"), None, None),
            P(("groups", "dev"), None),
            P(("groups", "dev"), None),
            P(("groups", "dev")),
            P("dev", None),
            P(),
            P(None, "dev"),
            P("dev", None),
            P(None, "dev"),
            P("dev", None),
            P(("groups", "dev"), None),
            P(("groups", "dev"), None),
        ),
        out_specs=P(("groups", "dev"), None),
        check_vma=False,
    )
```

```python
import functools
import math

import jax
import jax.numpy as jnp
from jax import lax
from jax.experimental import pallas as pl
from jax.experimental.pallas import tpu as pltpu
from jax.sharding import PartitionSpec as P

EXPERTS = 4
CHUNKS = 4
F32 = jnp.float32
BF16 = jnp.bfloat16


def layer_kernel(
    n,
    residual,
    queries,
    key_new,
    value_new,
    lengths,
    gain,
    ids,
    gates,
    key_hbm,
    value_hbm,
    out_hbm,
    sup_hbm,
    sdown_hbm,
    eup_hbm,
    edown_hbm,
    mixed,
    keys,
    values,
    out_w,
    sup_w,
    sdown_w,
    eup_w,
    edown_w,
    q_stage,
    c_stage,
    c_send,
    c_recv,
    g_recv,
    lhs_stage,
    g_stage,
    t_stage,
    s1a,
    r1a,
    s2a,
    r2a,
    s1b,
    r1b,
    s2b,
    r2b,
    own_total,
    hidden,
    normed,
    n_stage,
    load_sem,
    c_send_sem,
    c_recv_sem,
    g_send_sem,
    g_recv_sem,
    s1_sem,
    r1_sem,
    s2_sem,
    r2_sem,
    n_send_sem,
    n_recv_sem,
    f_send_sem,
    f_recv_sem,
):
    rows, width = residual.shape
    head_dim = keys.shape[2]
    heads = queries.shape[1] // head_dim
    per = heads // n
    chips = n // 2
    half = chips * rows
    total_rows = 2 * half
    chunk = width // CHUNKS
    me = lax.axis_index("dev")
    core = lax.rem(me, 2)
    chip = lax.div(me, 2)
    partner = me + 1 - 2 * core

    def cols(j):
        return pl.ds(j * chunk, chunk)

    def place(s):
        return (s % 2) * half + (s // 2) * rows

    loads = []
    for src, dst in (
        (key_hbm, keys),
        (value_hbm, values),
        (out_hbm, out_w),
        (sup_hbm, sup_w),
        (eup_hbm, eup_w),
        (sdown_hbm, sdown_w),
        (edown_hbm, edown_w),
    ):
        load = pltpu.make_async_copy(src, dst, load_sem.at[len(loads)])
        load.start()
        loads.append(load)

    barrier = pltpu.get_barrier_semaphore()

    def greet(o, carry):
        pl.semaphore_signal(
            barrier,
            inc=1,
            device_id={"dev": lax.rem(me + o, n)},
            device_id_type=pl.DeviceIdType.MESH,
        )
        return carry

    lax.fori_loop(1, n, greet, 0)

    def remote(src, dst, send, recv, device):
        return pltpu.make_async_remote_copy(
            src_ref=src,
            dst_ref=dst,
            send_sem=send,
            recv_sem=recv,
            device_id={"dev": device},
            device_id_type=pl.DeviceIdType.MESH,
        )

    lane = lax.broadcasted_iota(jnp.int32, (rows, 128), 1)
    table = jnp.zeros((rows, 128), F32)
    for k in range(ids.shape[1]):
        table = table + jnp.where(lane == ids[:, k : k + 1], gates[:, k : k + 1], 0.0)
    g_recv[pl.ds(me, 1)] = table[None]

    for h in range(heads):
        x = queries[:, h * head_dim : (h + 1) * head_dim].astype(F32)
        for r in range(rows):
            q_stage[r, h : h + 1, :] = x[r : r + 1]
    loads[0].wait()
    loads[1].wait()
    factor = 1.0 / math.sqrt(head_dim)
    for r in range(rows):
        q32 = q_stage[r]
        scores = (
            lax.dot_general(
                q32.astype(BF16), keys[r], (((1,), (1,)), ((), ())), preferred_element_type=F32
            )
            * factor
        )
        visible = lax.broadcasted_iota(jnp.int32, scores.shape, 1) < lengths[r]
        scores = jnp.where(visible, scores, -1e30)
        own = (
            jnp.sum(q32 * key_new[r : r + 1, :].astype(F32), axis=1, keepdims=True) * factor
        )
        top = jnp.maximum(jnp.max(scores, axis=1, keepdims=True), own)
        raised = jnp.where(visible, jnp.exp(scores - top), 0.0)
        raised_new = jnp.exp(own - top)
        denominator = jnp.sum(raised, axis=1, keepdims=True) + raised_new
        probs = (raised / denominator).astype(BF16)
        probs_new = (raised_new / denominator).astype(BF16).astype(F32)
        context = jnp.dot(probs, values[r], preferred_element_type=F32)
        context = context + probs_new * value_new[r : r + 1, :].astype(F32)
        q_stage[r] = context
    for d in range(n):
        for r in range(rows):
            c_stage[d, r * per : (r + 1) * per, :] = q_stage[r, d * per : (d + 1) * per, :]
    for d in range(n):
        c_send[d] = c_stage[d].astype(BF16)
    c_recv[pl.ds(me, 1)] = c_send[pl.ds(me, 1)]

    pl.semaphore_wait(barrier, n - 1)

    def c_copy(o):
        to = lax.rem(me + o, n)
        return remote(c_send.at[to], c_recv.at[me], c_send_sem, c_recv_sem.at[me], to)

    def g_copy(o):
        to = lax.rem(me + o, n)
        return remote(g_recv.at[me], g_recv.at[me], g_send_sem, g_recv_sem.at[me], to)

    for o in range(1, n):
        c_copy(o).start()
    for o in range(1, n):
        g_copy(o).start()
    for o in range(1, n):
        s = lax.rem(me + o, n)
        remote(c_recv.at[s], c_recv.at[s], c_send_sem, c_recv_sem.at[s], s).wait_recv()

    for s in range(n):
        x = c_recv[s].astype(F32)
        for r in range(rows):
            for h in range(per):
                lhs_stage[
                    place(s) + r : place(s) + r + 1, h * head_dim : (h + 1) * head_dim
                ] = x[r * per + h : r * per + h + 1]
    lhs = lhs_stage[...].astype(BF16)

    def first_stage(j, part, s1, r1, sem_at):
        part_a, part_b = part[:half], part[half:]
        s1[:, cols(j)] = jnp.where(core == 0, part_b, part_a).astype(BF16)
        copy = remote(
            s1.at[:, cols(j)],
            r1.at[:, cols(j)],
            s1_sem.at[sem_at, j],
            r1_sem.at[sem_at, j],
            partner,
        )
        copy.start()
        t_stage[:, cols(j)] = jnp.where(core == 0, part_a, part_b)
        return copy

    def second_copy(j, o, s2, r2, sem_at):
        to = lax.rem(chip + o, chips)
        return remote(
            s2.at[to, :, cols(j)],
            r2.at[chip, :, cols(j)],
            s2_sem.at[sem_at],
            r2_sem.at[sem_at, j, chip],
            2 * to + core,
        )

    def second_stage(j, copy, s2, r1, r2, sem_at):
        copy.wait_recv()
        t_stage[:, cols(j)] = t_stage[:, cols(j)] + r1[:, cols(j)].astype(F32)
        for c in range(chips):
            x = t_stage[c * rows : (c + 1) * rows, cols(j)]
            s2[c, :, cols(j)] = x.astype(BF16)
        for o in range(1, chips):
            second_copy(j, o, s2, r2, sem_at).start()

    def gathered(j, s2, r2, sem_at):
        x = s2[chip, :, cols(j)].astype(F32)
        for o in range(1, chips):
            c = lax.rem(chip + o, chips)
            remote(
                r2.at[c, :, cols(j)],
                r2.at[c, :, cols(j)],
                s2_sem.at[sem_at],
                r2_sem.at[sem_at, j, c],
                2 * c + core,
            ).wait_recv()
            x = x + r2[c, :, cols(j)].astype(F32)
        return x

    def reduce_scatter(make, s1, r1, s2, r2, sem_at):
        copies = []
        for j in range(CHUNKS):
            copies.append(first_stage(j, make(j), s1, r1, sem_at))
            if j >= 1:
                second_stage(j - 1, copies[j - 1], s2, r1, r2, sem_at)
        second_stage(CHUNKS - 1, copies[-1], s2, r1, r2, sem_at)

    loads[2].wait()
    reduce_scatter(
        lambda j: jnp.dot(lhs, out_w[:, cols(j)], preferred_element_type=F32), s1a, r1a, s2a, r2a, 0
    )

    square = jnp.zeros((rows, 1), F32)
    for j in range(CHUNKS):
        x = gathered(j, s2a, r2a, 0) + residual[:, cols(j)].astype(F32)
        hidden[:, cols(j)] = x
        square = square + jnp.sum(x * x, axis=1, keepdims=True)
    scale = lax.rsqrt(square / width + 1e-06)

    def n_copy(j, o):
        to = lax.rem(chip + o, chips)
        here = normed.at[core, chip, :, cols(j)]
        return remote(here, here, n_send_sem, n_recv_sem.at[j, chip], 2 * to + core)

    for j in range(CHUNKS):
        x = hidden[:, cols(j)] * scale * gain[cols(j)].astype(F32)[None, :]
        normed[pl.ds(core, 1), pl.ds(chip, 1), :, cols(j)] = x.astype(BF16)[None, None]
        for o in range(1, chips):
            n_copy(j, o).start()

    for o in range(1, n):
        s = lax.rem(me + o, n)
        remote(g_recv.at[s], g_recv.at[s], g_send_sem, g_recv_sem.at[s], s).wait_recv()
    for s in range(n):
        g_stage[place(s) : place(s) + rows, :] = g_recv[s]
    owner = lax.div(me, n // EXPERTS)
    lanes = lax.broadcasted_iota(jnp.int32, (total_rows, 128), 1)
    row_weight = jnp.sum(jnp.where(lanes == owner, g_stage[...], 0.0), axis=1, keepdims=True)

    def forward(j):
        block = normed.at[core, :, :, cols(j)]
        return remote(block, block, f_send_sem.at[j], f_recv_sem.at[j], partner)

    def arrive(j):
        for o in range(1, chips):
            c = lax.rem(chip + o, chips)
            there = normed.at[core, c, :, cols(j)]
            remote(there, there, n_send_sem, n_recv_sem.at[j, c], 2 * c + core).wait_recv()
        forward(j).start()

    loads[3].wait()
    loads[4].wait()
    shared = jnp.zeros((total_rows, sup_w.shape[0]), F32)
    routed = jnp.zeros((total_rows, eup_w.shape[1]), F32)
    arrive(0)
    for j in range(CHUNKS):
        if j + 1 < CHUNKS:
            arrive(j + 1)
        other = normed.at[1 - core, :, :, cols(j)]
        remote(other, other, f_send_sem.at[j], f_recv_sem.at[j], partner).wait_recv()
        for s in range(n):
            n_stage[place(s) : place(s) + rows, :] = normed[s % 2, s // 2, :, cols(j)].astype(F32)
        left = n_stage[...].astype(BF16)
        shared = shared + lax.dot_general(
            left, sup_w[:, cols(j)], (((1,), (1,)), ((), ())), preferred_element_type=F32
        )
        routed = routed + jnp.dot(left, eup_w[cols(j), :], preferred_element_type=F32)

    shared_act = (shared / (1.0 + jnp.exp(-shared))).astype(BF16)
    routed_act = (routed / (1.0 + jnp.exp(-routed))).astype(BF16)

    loads[5].wait()
    loads[6].wait()
    reduce_scatter(
        lambda j: jnp.dot(shared_act, sdown_w[:, cols(j)], preferred_element_type=F32)
        + row_weight * jnp.dot(routed_act, edown_w[:, cols(j)], preferred_element_type=F32),
        s1b,
        r1b,
        s2b,
        r2b,
        1,
    )
    for j in range(CHUNKS):
        mixed[:, cols(j)] = (hidden[:, cols(j)] + gathered(j, s2b, r2b, 1)).astype(BF16)

    for o in range(1, n):
        c_copy(o).wait_send()
        g_copy(o).wait_send()
    for j in range(CHUNKS):
        forward(j).wait_send()
        for s1, r1, s2, r2, sem_at in ((s1a, r1a, s2a, r2a, 0), (s1b, r1b, s2b, r2b, 1)):
            remote(
                s1.at[:, cols(j)],
                r1.at[:, cols(j)],
                s1_sem.at[sem_at, j],
                r1_sem.at[sem_at, j],
                partner,
            ).wait_send()
            for o in range(1, chips):
                second_copy(j, o, s2, r2, sem_at).wait_send()
        for o in range(1, chips):
            n_copy(j, o).wait_send()


def shards(
    residual,
    queries,
    key_cache,
    value_cache,
    key_new,
    value_new,
    lengths,
    out_weight,
    norm_gain,
    shared_up,
    shared_down,
    expert_up,
    expert_down,
    expert_ids,
    expert_gates,
):
    n = lax.axis_size("dev")
    rows, width = residual.shape
    head_dim = key_cache.shape[2]
    heads = queries.shape[1] // head_dim
    per = heads // n
    chips = n // 2
    half = chips * rows
    chunk = width // CHUNKS
    vmem = pl.BlockSpec(memory_space=pltpu.VMEM)
    smem = pl.BlockSpec(memory_space=pltpu.SMEM)
    hbm = pl.BlockSpec(memory_space=pl.ANY)
    dma = pltpu.SemaphoreType.DMA
    stage_pair = [
        pltpu.VMEM((half, width), BF16),
        pltpu.VMEM((half, width), BF16),
        pltpu.VMEM((chips, rows, width), BF16),
        pltpu.VMEM((chips, rows, width), BF16),
    ]
    return pl.pallas_call(
        functools.partial(layer_kernel, n),
        out_shape=jax.ShapeDtypeStruct((rows, width), BF16),
        in_specs=[vmem] * 4 + [smem] + [vmem] * 3 + [hbm] * 7,
        out_specs=vmem,
        scratch_shapes=[
            pltpu.VMEM(a.shape, BF16)
            for a in (
                key_cache,
                value_cache,
                out_weight,
                shared_up.T,
                shared_down,
                expert_up,
                expert_down,
            )
        ]
        + [
            pltpu.VMEM((rows, heads, head_dim), F32),
            pltpu.VMEM((n, rows * per, head_dim), F32),
            pltpu.VMEM((n, rows * per, head_dim), BF16),
            pltpu.VMEM((n, rows * per, head_dim), BF16),
            pltpu.VMEM((n, rows, 128), F32),
            pltpu.VMEM((2 * half, per * head_dim), F32),
            pltpu.VMEM((2 * half, 128), F32),
            pltpu.VMEM((half, width), F32),
        ]
        + stage_pair
        + stage_pair
        + [
            pltpu.VMEM((rows, width), F32),
            pltpu.VMEM((rows, width), F32),
            pltpu.VMEM((2, chips, rows, width), BF16),
            pltpu.VMEM((2 * half, chunk), F32),
            dma((7,)),
            dma,
            dma((n,)),
            dma,
            dma((n,)),
            dma((2, CHUNKS)),
            dma((2, CHUNKS)),
            dma((2,)),
            dma((2, CHUNKS, chips)),
            dma,
            dma((CHUNKS, chips)),
            dma((CHUNKS,)),
            dma((CHUNKS,)),
        ],
        compiler_params=pltpu.CompilerParams(
            collective_id=0, has_side_effects=True, vmem_limit_bytes=63 * 1024 * 1024
        ),
        name="layer",
    )(
        residual,
        queries,
        key_new,
        value_new,
        lengths,
        norm_gain,
        expert_ids,
        expert_gates,
        key_cache,
        value_cache,
        out_weight,
        shared_up.T,
        shared_down,
        expert_up,
        expert_down,
    )


def solution(mesh):
    return jax.shard_map(
        shards,
        mesh=mesh,
        in_specs=(
            P(("groups", "dev"), None),
            P(("groups", "dev"), None),
            P(("groups", "dev"), None, None),
            P(("groups", "dev"), None, None),
            P(("groups", "dev"), None),
            P(("groups", "dev"), None),
            P(("groups", "dev")),
            P("dev", None),
            P(),
            P(None, "dev"),
            P("dev", None),
            P(None, "dev"),
            P("dev", None),
            P(("groups", "dev"), None),
            P(("groups", "dev"), None),
        ),
        out_specs=P(("groups", "dev"), None),
        check_vma=False,
    )
```

```python
import functools
import math

import jax
import jax.numpy as jnp
from jax import lax
from jax.experimental import pallas as pl
from jax.experimental.pallas import tpu as pltpu
from jax.sharding import PartitionSpec as P

EXPERTS = 4
CHUNKS = 4
F32 = jnp.float32
BF16 = jnp.bfloat16


def layer_kernel(
    n,
    residual,
    queries,
    key_new,
    value_new,
    lengths,
    gain,
    ids,
    gates,
    key_hbm,
    value_hbm,
    out_hbm,
    sup_hbm,
    sdown_hbm,
    eup_hbm,
    edown_hbm,
    mixed,
    keys,
    values,
    out_w,
    sup_w,
    sdown_w,
    eup_w,
    edown_w,
    q_stage,
    c_stage,
    c_send,
    c_recv,
    g_recv,
    lhs_stage,
    g_stage,
    t_stage,
    s1a,
    r1a,
    s2a,
    r2a,
    s1b,
    r1b,
    s2b,
    r2b,
    own_total,
    hidden,
    normed,
    n_stage,
    load_sem,
    c_send_sem,
    c_recv_sem,
    g_send_sem,
    g_recv_sem,
    s1_sem,
    r1_sem,
    s2_sem,
    r2_sem,
    n_send_sem,
    n_recv_sem,
    f_send_sem,
    f_recv_sem,
):
    rows, width = residual.shape
    head_dim = keys.shape[2]
    heads = queries.shape[1] // head_dim
    per = heads // n
    chips = n // 2
    half = chips * rows
    total_rows = 2 * half
    chunk = width // CHUNKS
    me = lax.axis_index("dev")
    core = lax.rem(me, 2)
    chip = lax.div(me, 2)
    partner = me + 1 - 2 * core

    def cols(j):
        return pl.ds(j * chunk, chunk)

    def place(s):
        return (s % 2) * half + (s // 2) * rows

    loads = []
    for src, dst in (
        (key_hbm, keys),
        (value_hbm, values),
        (out_hbm, out_w),
        (sup_hbm, sup_w),
        (eup_hbm, eup_w),
        (sdown_hbm, sdown_w),
        (edown_hbm, edown_w),
    ):
        loads.append(pltpu.make_async_copy(src, dst, load_sem.at[len(loads)]))
    for load in loads[:3]:
        load.start()

    barrier = pltpu.get_barrier_semaphore()

    def greet(o, carry):
        pl.semaphore_signal(
            barrier,
            inc=1,
            device_id={"dev": lax.rem(me + o, n)},
            device_id_type=pl.DeviceIdType.MESH,
        )
        return carry

    lax.fori_loop(1, n, greet, 0)

    def remote(src, dst, send, recv, device):
        return pltpu.make_async_remote_copy(
            src_ref=src,
            dst_ref=dst,
            send_sem=send,
            recv_sem=recv,
            device_id={"dev": device},
            device_id_type=pl.DeviceIdType.MESH,
        )

    lane = lax.broadcasted_iota(jnp.int32, (rows, 128), 1)
    table = jnp.zeros((rows, 128), F32)
    for k in range(ids.shape[1]):
        table = table + jnp.where(lane == ids[:, k : k + 1], gates[:, k : k + 1], 0.0)
    g_recv[pl.ds(me, 1)] = table[None]

    for h in range(heads):
        x = queries[:, h * head_dim : (h + 1) * head_dim].astype(F32)
        for r in range(rows):
            q_stage[r, h : h + 1, :] = x[r : r + 1]
    loads[0].wait()
    loads[1].wait()
    factor = 1.0 / math.sqrt(head_dim)
    for r in range(rows):
        q32 = q_stage[r]
        scores = (
            lax.dot_general(
                q32.astype(BF16), keys[r], (((1,), (1,)), ((), ())), preferred_element_type=F32
            )
            * factor
        )
        visible = lax.broadcasted_iota(jnp.int32, scores.shape, 1) < lengths[r]
        scores = jnp.where(visible, scores, -1e30)
        own = (
            jnp.sum(q32 * key_new[r : r + 1, :].astype(F32), axis=1, keepdims=True) * factor
        )
        top = jnp.maximum(jnp.max(scores, axis=1, keepdims=True), own)
        raised = jnp.where(visible, jnp.exp(scores - top), 0.0)
        raised_new = jnp.exp(own - top)
        denominator = jnp.sum(raised, axis=1, keepdims=True) + raised_new
        probs = (raised / denominator).astype(BF16)
        probs_new = (raised_new / denominator).astype(BF16).astype(F32)
        context = jnp.dot(probs, values[r], preferred_element_type=F32)
        context = context + probs_new * value_new[r : r + 1, :].astype(F32)
        q_stage[r] = context
    for d in range(n):
        for r in range(rows):
            c_stage[d, r * per : (r + 1) * per, :] = q_stage[r, d * per : (d + 1) * per, :]
    for d in range(n):
        c_send[d] = c_stage[d].astype(BF16)
    c_recv[pl.ds(me, 1)] = c_send[pl.ds(me, 1)]

    pl.semaphore_wait(barrier, n - 1)

    def c_copy(o):
        to = lax.rem(me + o, n)
        return remote(c_send.at[to], c_recv.at[me], c_send_sem, c_recv_sem.at[me], to)

    def g_copy(o):
        to = lax.rem(me + o, n)
        return remote(g_recv.at[me], g_recv.at[me], g_send_sem, g_recv_sem.at[me], to)

    for o in range(1, n):
        c_copy(o).start()
    for o in range(1, n):
        g_copy(o).start()
    loads[2].wait()
    for load in loads[3:]:
        load.start()
    for o in range(1, n):
        s = lax.rem(me + o, n)
        remote(c_recv.at[s], c_recv.at[s], c_send_sem, c_recv_sem.at[s], s).wait_recv()

    for s in range(n):
        x = c_recv[s].astype(F32)
        for r in range(rows):
            for h in range(per):
                lhs_stage[
                    place(s) + r : place(s) + r + 1, h * head_dim : (h + 1) * head_dim
                ] = x[r * per + h : r * per + h + 1]
    lhs = lhs_stage[...].astype(BF16)

    def first_stage(j, part, s1, r1, sem_at):
        part_a, part_b = part[:half], part[half:]
        s1[:, cols(j)] = jnp.where(core == 0, part_b, part_a).astype(BF16)
        copy = remote(
            s1.at[:, cols(j)],
            r1.at[:, cols(j)],
            s1_sem.at[sem_at, j],
            r1_sem.at[sem_at, j],
            partner,
        )
        copy.start()
        t_stage[:, cols(j)] = jnp.where(core == 0, part_a, part_b)
        return copy

    def second_copy(j, o, s2, r2, sem_at):
        to = lax.rem(chip + o, chips)
        return remote(
            s2.at[to, :, cols(j)],
            r2.at[chip, :, cols(j)],
            s2_sem.at[sem_at],
            r2_sem.at[sem_at, j, chip],
            2 * to + core,
        )

    def second_stage(j, copy, s2, r1, r2, sem_at):
        copy.wait_recv()
        t_stage[:, cols(j)] = t_stage[:, cols(j)] + r1[:, cols(j)].astype(F32)
        for c in range(chips):
            x = t_stage[c * rows : (c + 1) * rows, cols(j)]
            s2[c, :, cols(j)] = x.astype(BF16)
        for o in range(1, chips):
            second_copy(j, o, s2, r2, sem_at).start()

    def gathered(j, s2, r2, sem_at):
        x = s2[chip, :, cols(j)].astype(F32)
        for o in range(1, chips):
            c = lax.rem(chip + o, chips)
            remote(
                r2.at[c, :, cols(j)],
                r2.at[c, :, cols(j)],
                s2_sem.at[sem_at],
                r2_sem.at[sem_at, j, c],
                2 * c + core,
            ).wait_recv()
            x = x + r2[c, :, cols(j)].astype(F32)
        return x

    def reduce_scatter(make, s1, r1, s2, r2, sem_at):
        copies = []
        for j in range(CHUNKS):
            copies.append(first_stage(j, make(j), s1, r1, sem_at))
            if j >= 1:
                second_stage(j - 1, copies[j - 1], s2, r1, r2, sem_at)
        second_stage(CHUNKS - 1, copies[-1], s2, r1, r2, sem_at)

    reduce_scatter(
        lambda j: jnp.dot(lhs, out_w[:, cols(j)], preferred_element_type=F32), s1a, r1a, s2a, r2a, 0
    )

    square = jnp.zeros((rows, 1), F32)
    for j in range(CHUNKS):
        x = gathered(j, s2a, r2a, 0) + residual[:, cols(j)].astype(F32)
        hidden[:, cols(j)] = x
        square = square + jnp.sum(x * x, axis=1, keepdims=True)
    scale = lax.rsqrt(square / width + 1e-06)

    def n_copy(j, o):
        to = lax.rem(chip + o, chips)
        here = normed.at[core, chip, :, cols(j)]
        return remote(here, here, n_send_sem, n_recv_sem.at[j, chip], 2 * to + core)

    for j in range(CHUNKS):
        x = hidden[:, cols(j)] * scale * gain[cols(j)].astype(F32)[None, :]
        normed[pl.ds(core, 1), pl.ds(chip, 1), :, cols(j)] = x.astype(BF16)[None, None]
        for o in range(1, chips):
            n_copy(j, o).start()

    for o in range(1, n):
        s = lax.rem(me + o, n)
        remote(g_recv.at[s], g_recv.at[s], g_send_sem, g_recv_sem.at[s], s).wait_recv()
    for s in range(n):
        g_stage[place(s) : place(s) + rows, :] = g_recv[s]
    owner = lax.div(me, n // EXPERTS)
    lanes = lax.broadcasted_iota(jnp.int32, (total_rows, 128), 1)
    row_weight = jnp.sum(jnp.where(lanes == owner, g_stage[...], 0.0), axis=1, keepdims=True)

    def forward(j):
        block = normed.at[core, :, :, cols(j)]
        return remote(block, block, f_send_sem.at[j], f_recv_sem.at[j], partner)

    def arrive(j):
        for o in range(1, chips):
            c = lax.rem(chip + o, chips)
            there = normed.at[core, c, :, cols(j)]
            remote(there, there, n_send_sem, n_recv_sem.at[j, c], 2 * c + core).wait_recv()
        forward(j).start()

    loads[3].wait()
    loads[4].wait()
    shared = jnp.zeros((total_rows, sup_w.shape[0]), F32)
    routed = jnp.zeros((total_rows, eup_w.shape[1]), F32)
    arrive(0)
    for j in range(CHUNKS):
        if j + 1 < CHUNKS:
            arrive(j + 1)
        other = normed.at[1 - core, :, :, cols(j)]
        remote(other, other, f_send_sem.at[j], f_recv_sem.at[j], partner).wait_recv()
        for s in range(n):
            n_stage[place(s) : place(s) + rows, :] = normed[s % 2, s // 2, :, cols(j)].astype(F32)
        left = n_stage[...].astype(BF16)
        shared = shared + lax.dot_general(
            left, sup_w[:, cols(j)], (((1,), (1,)), ((), ())), preferred_element_type=F32
        )
        routed = routed + jnp.dot(left, eup_w[cols(j), :], preferred_element_type=F32)

    shared_act = (shared / (1.0 + jnp.exp(-shared))).astype(BF16)
    routed_act = (routed / (1.0 + jnp.exp(-routed))).astype(BF16)

    loads[5].wait()
    loads[6].wait()
    reduce_scatter(
        lambda j: jnp.dot(shared_act, sdown_w[:, cols(j)], preferred_element_type=F32)
        + row_weight * jnp.dot(routed_act, edown_w[:, cols(j)], preferred_element_type=F32),
        s1b,
        r1b,
        s2b,
        r2b,
        1,
    )
    for j in range(CHUNKS):
        mixed[:, cols(j)] = (hidden[:, cols(j)] + gathered(j, s2b, r2b, 1)).astype(BF16)

    for o in range(1, n):
        c_copy(o).wait_send()
        g_copy(o).wait_send()
    for j in range(CHUNKS):
        forward(j).wait_send()
        for s1, r1, s2, r2, sem_at in ((s1a, r1a, s2a, r2a, 0), (s1b, r1b, s2b, r2b, 1)):
            remote(
                s1.at[:, cols(j)],
                r1.at[:, cols(j)],
                s1_sem.at[sem_at, j],
                r1_sem.at[sem_at, j],
                partner,
            ).wait_send()
            for o in range(1, chips):
                second_copy(j, o, s2, r2, sem_at).wait_send()
        for o in range(1, chips):
            n_copy(j, o).wait_send()


def shards(
    residual,
    queries,
    key_cache,
    value_cache,
    key_new,
    value_new,
    lengths,
    out_weight,
    norm_gain,
    shared_up,
    shared_down,
    expert_up,
    expert_down,
    expert_ids,
    expert_gates,
):
    n = lax.axis_size("dev")
    rows, width = residual.shape
    head_dim = key_cache.shape[2]
    heads = queries.shape[1] // head_dim
    per = heads // n
    chips = n // 2
    half = chips * rows
    chunk = width // CHUNKS
    vmem = pl.BlockSpec(memory_space=pltpu.VMEM)
    smem = pl.BlockSpec(memory_space=pltpu.SMEM)
    hbm = pl.BlockSpec(memory_space=pl.ANY)
    dma = pltpu.SemaphoreType.DMA
    stage_pair = [
        pltpu.VMEM((half, width), BF16),
        pltpu.VMEM((half, width), BF16),
        pltpu.VMEM((chips, rows, width), BF16),
        pltpu.VMEM((chips, rows, width), BF16),
    ]
    return pl.pallas_call(
        functools.partial(layer_kernel, n),
        out_shape=jax.ShapeDtypeStruct((rows, width), BF16),
        in_specs=[vmem] * 4 + [smem] + [vmem] * 3 + [hbm] * 7,
        out_specs=vmem,
        scratch_shapes=[
            pltpu.VMEM(a.shape, BF16)
            for a in (
                key_cache,
                value_cache,
                out_weight,
                shared_up.T,
                shared_down,
                expert_up,
                expert_down,
            )
        ]
        + [
            pltpu.VMEM((rows, heads, head_dim), F32),
            pltpu.VMEM((n, rows * per, head_dim), F32),
            pltpu.VMEM((n, rows * per, head_dim), BF16),
            pltpu.VMEM((n, rows * per, head_dim), BF16),
            pltpu.VMEM((n, rows, 128), F32),
            pltpu.VMEM((2 * half, per * head_dim), F32),
            pltpu.VMEM((2 * half, 128), F32),
            pltpu.VMEM((half, width), F32),
        ]
        + stage_pair
        + stage_pair
        + [
            pltpu.VMEM((rows, width), F32),
            pltpu.VMEM((rows, width), F32),
            pltpu.VMEM((2, chips, rows, width), BF16),
            pltpu.VMEM((2 * half, chunk), F32),
            dma((7,)),
            dma,
            dma((n,)),
            dma,
            dma((n,)),
            dma((2, CHUNKS)),
            dma((2, CHUNKS)),
            dma((2,)),
            dma((2, CHUNKS, chips)),
            dma,
            dma((CHUNKS, chips)),
            dma((CHUNKS,)),
            dma((CHUNKS,)),
        ],
        compiler_params=pltpu.CompilerParams(
            collective_id=0, has_side_effects=True, vmem_limit_bytes=63 * 1024 * 1024
        ),
        name="layer",
    )(
        residual,
        queries,
        key_new,
        value_new,
        lengths,
        norm_gain,
        expert_ids,
        expert_gates,
        key_cache,
        value_cache,
        out_weight,
        shared_up.T,
        shared_down,
        expert_up,
        expert_down,
    )


def solution(mesh):
    return jax.shard_map(
        shards,
        mesh=mesh,
        in_specs=(
            P(("groups", "dev"), None),
            P(("groups", "dev"), None),
            P(("groups", "dev"), None, None),
            P(("groups", "dev"), None, None),
            P(("groups", "dev"), None),
            P(("groups", "dev"), None),
            P(("groups", "dev")),
            P("dev", None),
            P(),
            P(None, "dev"),
            P("dev", None),
            P(None, "dev"),
            P("dev", None),
            P(("groups", "dev"), None),
            P(("groups", "dev"), None),
        ),
        out_specs=P(("groups", "dev"), None),
        check_vma=False,
    )
```
